256 devices in a mesh: leaf: 64 (over z, y, core), samp: 4 (over x).
Axes of the slice: x: 4, y: 4, z: 8, core: 2. Of those that a mesh axis runs over, the one named last changes fastest.
Arguments:
- patterns: float32 [2048, 4, 72, 256], P(('leaf', 'samp')), may hold values from -6 to 6
- child_code: int32 [2048], P(('leaf', 'samp')), may hold values from -1 to 7, as said below
- box_codes: int32 [256], replicated, may hold values from 0 to 511, as said below
- shift_scale: float32 [2], replicated, may hold values from 8 to 40
- theta_lower: float32 [144, 4], replicated, may hold values from -3 to 3
- phi_lower: float32 [512, 4], replicated, may hold values from -3 to 3
- theta_upper: float32 [288, 4], replicated, may hold values from -3 to 3
- phi_upper: float32 [1024, 4], replicated, may hold values from -3 to 3
- far_lists: int32 [64, 8], replicated, may hold values from -1 to 63, as said below
- far_kinds: int32 [64, 8], replicated, may hold values from 0 to 63
- translators: float32 [64, 2, 288, 1024], P(None, None, 'samp', 'leaf'), may hold values from -0.12 to 0.12
Outputs:
- incoming: float32 [2048, 4, 72, 256], P(('leaf', 'samp'))
The draws below stay inside these ranges and needn't reach their ends.
Inputs may be any that keep to these rules, and one draw needn't show every extreme that they name: `child_code`: in each group of 8 slots of a level-6 box the used slots come first, with distinct octants in increasing order, and the others hold -1; a box uses 1 to 8 slots, and some box uses all 8. `box_codes`: strictly increasing. `far_lists`: in each row the entries other than -1 come first; no entry names the row's own box.
All inputs are finite; a program needn't handle non-finite values.
Results may differ from the reference program's by a relative error of at most 0.0003.
Values sent between devices are 32-bit elements; how exact they have to be, the bound alone decides.
A program may use at most 192 MiB of HBM per device.

```python
import math
import jax
import jax.numpy as jnp
from jax import lax

NTH7 = 72
NPH7 = 256
TAPS = 4
KIDS = 8
NLIST = 8
NTYPE = 64
NTH6 = 144
NPH6 = 512
NTH5 = 288
NPH5 = 1024
NB6 = 256
NB5 = 64


def draw_child_code(key, part):
    first, second, third = jax.random.split(key, 3)
    counts = jax.random.randint(first, (NB6,), 1, KIDS + 1)
    full_box = jax.random.randint(second, (), 0, NB6)
    counts = jnp.where(jnp.arange(NB6) == full_box, KIDS, counts)
    scores = jax.random.randint(third, (NB6, KIDS), 0, 1 << 20)
    order = jnp.argsort(scores, axis=1, stable=True).astype(jnp.int32)
    slot_index = jnp.arange(KIDS, dtype=jnp.int32)[None, :]
    chosen = jnp.where(slot_index < counts[:, None], order, KIDS)
    chosen = jnp.sort(chosen, axis=1)
    codes = jnp.where(chosen == KIDS, -1, chosen)
    return codes.reshape(NB6 * KIDS).astype(jnp.int32)


def draw_box_codes(key, part):
    inner = jax.random.permutation(key, KIDS * NB5 - 2)[:NB6 - 2] + 1
    picked = jnp.concatenate([jnp.zeros((1,), jnp.int32), inner.astype(jnp.int32), jnp.full((1,), KIDS * NB5 - 1, jnp.int32)])
    return jnp.sort(picked).astype(jnp.int32)


def draw_far_lists(key, part):
    first, second, third = jax.random.split(key, 3)
    lengths = jax.random.randint(first, (NB5,), 1, NLIST + 1)
    full_row = jax.random.randint(second, (), 0, NB5)
    rows = jnp.arange(NB5, dtype=jnp.int32)
    lengths = jnp.where(rows == full_row, NLIST, lengths)
    lengths = jnp.where(rows == (full_row + 1) % NB5, 1, lengths)
    offsets = jax.random.randint(third, (NB5, NLIST), 1, NB5)
    sources = (rows[:, None] + offsets) % NB5
    first_entry = (rows[:, None] == 0) & (jnp.arange(NLIST)[None, :] == 0)
    sources = jnp.where(first_entry, NB5 - 1, sources)
    lists = jnp.where(jnp.arange(NLIST)[None, :] < lengths[:, None], sources, -1)
    return lists.astype(jnp.int32)


def plant(drawn, own_key, smallest, largest):
    dims = drawn.shape
    place = [jax.random.randint(jax.random.fold_in(own_key, axis), (), 0, dims[axis]) for axis in range(len(dims))]
    drawn = drawn.at[tuple(place)].set(smallest)
    longest = dims.index(max(dims))
    place[longest] = (place[longest] + 1) % dims[longest]
    return drawn.at[tuple(place)].set(largest)


def block_levels(own_key, dims, pieces, low, top_value):
    loudness, own = 1.0, jax.random.fold_in(own_key, 6)
    for dim, blocks in pieces:
        heights = jnp.exp(jax.random.uniform(jax.random.fold_in(own, dim), (blocks,), jnp.float32, low / len(pieces), top_value / len(pieces)))
        loudness = loudness * jnp.repeat(heights, dims[dim] // blocks).reshape([-1 if axis == dim else 1 for axis in range(len(dims))])
    return loudness


def centred(own_key, shape, scale, bound, cuts=(), held_as=jnp.bfloat16):
    drawn = scale * jax.random.normal(own_key, shape, jnp.float32)
    if cuts:
        drawn = drawn * block_levels(own_key, shape, cuts, -0.22, 0.18)
    return jnp.clip(drawn, -bound, bound).astype(held_as)


def setup_inputs(seed: int = 0) -> dict:
    key_list = jax.random.split(jax.random.key(seed), 12)
    patterns = centred(key_list[0], (NB6 * KIDS, 4, NTH7, NPH7), 1.0, 6.0, ((0, 256),), jnp.float32)
    child_code = draw_child_code(jax.random.fold_in(key_list[11], 71), 0)
    box_codes = draw_box_codes(jax.random.fold_in(key_list[11], 71), 0)
    shift_scale = jnp.clip(jnp.exp(jax.random.uniform(key_list[3], (2,), jnp.float32, math.log(8.0), math.log(40.0))), 8.0, 40.0)
    theta_lower = centred(key_list[4], (NTH6, TAPS), 0.5, 3.0, (), jnp.float32)
    phi_lower = centred(key_list[5], (NPH6, TAPS), 0.5, 3.0, (), jnp.float32)
    theta_upper = centred(key_list[6], (NTH5, TAPS), 0.5, 3.0, (), jnp.float32)
    phi_upper = centred(key_list[7], (NPH5, TAPS), 0.5, 3.0, (), jnp.float32)
    far_lists = draw_far_lists(jax.random.fold_in(key_list[11], 71), 0)
    far_kinds = plant(jax.random.randint(key_list[9], (NB5, NLIST), 0, NTYPE), jax.random.fold_in(key_list[9], 1), 0, NTYPE - 1).astype(jnp.int32)
    translators = centred(key_list[10], (NTYPE, 2, NTH5, NPH5), 0.02, 0.12, ((2, 4), (3, 64)), jnp.float32)
    return dict(patterns=patterns, child_code=child_code, box_codes=box_codes, shift_scale=shift_scale, theta_lower=theta_lower, phi_lower=phi_lower, theta_upper=theta_upper, phi_upper=phi_upper, far_lists=far_lists, far_kinds=far_kinds, translators=translators)


def raise_grid(field, weights, axis):
    bshape = [1] * field.ndim
    bshape[axis] = weights.shape[0]
    total = None
    for stencil in range(weights.shape[1]):
        moved = jnp.repeat(jnp.roll(field, 1 - stencil, axis=axis), 2, axis=axis)
        term = moved * weights[:, stencil].reshape(bshape)
        total = term if total is None else total + term
    return total


def lower_grid(field, weights, axis):
    width = field.shape[axis]
    bshape = [1] * field.ndim
    bshape[axis] = width
    split = list(field.shape[:axis]) + [width // 2, 2] + list(field.shape[axis + 1:])
    total = None
    for stencil in range(weights.shape[1]):
        paired = (field * weights[:, stencil].reshape(bshape)).reshape(split).sum(axis=axis + 1)
        term = jnp.roll(paired, stencil - 1, axis=axis)
        total = term if total is None else total + term
    return total


def phases(codes, kappa, theta_index, phi_index, theta_count, phi_count):
    theta = math.pi * (theta_index.astype(jnp.float32) + 0.5) / theta_count
    azimuth = 2.0 * math.pi * phi_index.astype(jnp.float32) / phi_count
    sign_x = (codes % 2).astype(jnp.float32) * 2.0 - 1.0
    sign_y = ((codes // 2) % 2).astype(jnp.float32) * 2.0 - 1.0
    sign_z = ((codes // 4) % 2).astype(jnp.float32) * 2.0 - 1.0
    sines = jnp.sin(theta)[:, None]
    along_x = sines * jnp.cos(azimuth)[None, :]
    along_y = sines * jnp.sin(azimuth)[None, :]
    along_z = jnp.cos(theta)[:, None] + 0.0 * azimuth[None, :]
    angle = kappa * (sign_x[:, None, None] * along_x + sign_y[:, None, None] * along_y + sign_z[:, None, None] * along_z)
    return jnp.cos(angle), jnp.sin(angle)


def rotate(field, cosine, sine):
    count, parts, height, width = field.shape
    grouped = field.reshape(count, 2, 2, height, width)
    real_part = grouped[:, :, 0]
    imag_part = grouped[:, :, 1]
    cosine = cosine[:, None]
    sine = sine[:, None]
    turned = jnp.stack([real_part * cosine - imag_part * sine, real_part * sine + imag_part * cosine], axis=2)
    return turned.reshape(field.shape)


def translate(upward, sources, selectors, operators):
    def accumulate(entry, total):
        source = lax.dynamic_index_in_dim(sources, entry, 1, keepdims=False)
        selector = lax.dynamic_index_in_dim(selectors, entry, 1, keepdims=False)
        valid = (source >= 0).astype(jnp.float32)
        picked = jnp.take(upward, jnp.maximum(source, 0), axis=0) * valid[:, None, None, None]
        chosen = jnp.take(operators, selector, axis=0)
        return total + rotate(picked, chosen[:, 0], chosen[:, 1])
    return lax.fori_loop(0, sources.shape[1], accumulate, jnp.zeros(upward.shape, jnp.float32))


def reference(patterns, child_code, box_codes, shift_scale, theta_lower, phi_lower, theta_upper, phi_upper, far_lists, far_kinds, translators):
    groups = patterns.reshape(NB6, KIDS, 4, NTH7, NPH7)
    codes = child_code.reshape(NB6, KIDS)
    parents = box_codes // KIDS
    octants = box_codes % KIDS
    theta_six = jnp.arange(NTH6, dtype=jnp.int32)
    phi_six = jnp.arange(NPH6, dtype=jnp.int32)
    theta_five = jnp.arange(NTH5, dtype=jnp.int32)
    phi_five = jnp.arange(NPH5, dtype=jnp.int32)

    def upward_one(total, item):
        group, code, parent, octant = item
        used = (code >= 0).astype(jnp.float32)
        fine = raise_grid(raise_grid(group, theta_lower, 2), phi_lower, 3)
        cosine, sine = phases(jnp.maximum(code, 0), shift_scale[0], theta_six, phi_six, NTH6, NPH6)
        middle = jnp.sum(rotate(fine, cosine, sine) * used[:, None, None, None], axis=0)
        lifted = raise_grid(raise_grid(middle[None], theta_upper, 2), phi_upper, 3)
        cos_five, sin_five = phases(octant[None], shift_scale[1], theta_five, phi_five, NTH5, NPH5)
        turned = rotate(lifted, cos_five, sin_five)[0]
        return total.at[parent].add(turned), None

    upward, unused = lax.scan(upward_one, jnp.zeros((NB5, 4, NTH5, NPH5), jnp.float32), (groups, codes, parents, octants))
    downward = translate(upward, far_lists, far_kinds, translators)

    def downward_one(item):
        code, parent, octant = item
        used = (code >= 0).astype(jnp.float32)
        cos_five, sin_five = phases(octant[None], shift_scale[1], theta_five, phi_five, NTH5, NPH5)
        split = rotate(downward[parent][None], cos_five, -sin_five)
        mid_down = lower_grid(lower_grid(split, theta_upper, 2), phi_upper, 3)
        cosine, sine = phases(jnp.maximum(code, 0), shift_scale[0], theta_six, phi_six, NTH6, NPH6)
        spread = rotate(jnp.broadcast_to(mid_down, (KIDS, 4, NTH6, NPH6)), cosine, -sine)
        coarse = lower_grid(lower_grid(spread, theta_lower, 2), phi_lower, 3)
        return coarse * used[:, None, None, None]

    incoming = lax.map(downward_one, (codes, parents, octants))
    return incoming.reshape(NB6 * KIDS, 4, NTH7, NPH7)
```

```python
import math

import jax
import jax.numpy as jnp
from jax import lax
from jax.sharding import PartitionSpec as P

KIDS = 8
HI = lax.Precision.HIGHEST


def iota(n):
    return lax.optimization_barrier(jnp.arange(n, dtype=jnp.int32))


def raise_matrix(weights, width):
    count = weights.shape[0]
    rows = iota(count)
    columns = iota(width)
    matrix = jnp.zeros((count, width), jnp.float32)
    for stencil in range(weights.shape[1]):
        source = (rows // 2 + stencil - 1) % width
        hits = (source[:, None] == columns[None, :]).astype(jnp.float32)
        matrix = matrix + hits * weights[:, stencil][:, None]
    return matrix


def block_matrix(weights, halo):
    count = weights.shape[0]
    rows = iota(count)
    columns = iota(halo)
    matrix = jnp.zeros((count, halo), jnp.float32)
    for stencil in range(weights.shape[1]):
        hits = ((rows // 2 + stencil)[:, None] == columns[None, :]).astype(jnp.float32)
        matrix = matrix + hits * weights[:, stencil][:, None]
    return matrix


def halo_picker(blocks, block, halo, width):
    b = iota(blocks)
    i = iota(halo)
    r = iota(width)
    place = (b[:, None] * block - 1 + i[None, :]) % width
    return (place[:, :, None] == r[None, None, :]).astype(jnp.float32)


def phases(codes, kappa, theta_index, phi_index, theta_count, phi_count):
    theta = math.pi * (theta_index.astype(jnp.float32) + 0.5) / theta_count
    azimuth = 2.0 * math.pi * phi_index.astype(jnp.float32) / phi_count
    sign_x = (codes % 2).astype(jnp.float32) * 2.0 - 1.0
    sign_y = (codes // 2 % 2).astype(jnp.float32) * 2.0 - 1.0
    sign_z = (codes // 4 % 2).astype(jnp.float32) * 2.0 - 1.0
    sines = jnp.sin(theta)[:, None]
    along_x = sines * jnp.cos(azimuth)[None, :]
    along_y = sines * jnp.sin(azimuth)[None, :]
    along_z = jnp.cos(theta)[:, None] + 0.0 * azimuth[None, :]
    angle = kappa * (
        sign_x[:, None, None] * along_x
        + sign_y[:, None, None] * along_y
        + sign_z[:, None, None] * along_z
    )
    return (jnp.cos(angle), jnp.sin(angle))


def rotate(field, cosine, sine):
    count = field.shape[0]
    rest = field.shape[2:]
    grouped = field.reshape((count, 2, 2) + rest)
    real_part = grouped[:, :, 0]
    imag_part = grouped[:, :, 1]
    cosine = cosine[:, None]
    sine = sine[:, None]
    turned = jnp.stack(
        [real_part * cosine - imag_part * sine, real_part * sine + imag_part * cosine], axis=2
    )
    return turned.reshape(field.shape)


def body(
    patterns,
    child_code,
    box_codes,
    shift_scale,
    theta_lower,
    phi_lower,
    theta_upper,
    phi_upper,
    far_lists,
    far_kinds,
    translators,
):
    slots, parts, rows_seven, cols_seven = patterns.shape
    rows_six, cols_six = 2 * rows_seven, 2 * cols_seven
    rows_five, cols_five = 4 * rows_seven, 4 * cols_seven
    n_samp = lax.axis_size("samp")
    n_leaf = lax.axis_size("leaf")
    samp = lax.axis_index("samp")
    leaf = lax.axis_index("leaf")
    block_rows_six = rows_six // n_samp
    block_cols_six = cols_six // n_leaf
    block_rows_five = 2 * block_rows_six
    block_cols_five = 2 * block_cols_six
    halo_rows = block_rows_six + 3
    halo_cols = block_cols_six + 3
    total_six = box_codes.shape[0]
    total_five = far_lists.shape[0]
    block_size = block_rows_five * block_cols_five

    used = (child_code >= 0).astype(jnp.float32)
    codes = jnp.maximum(child_code, 0)
    rows_lower = raise_matrix(theta_lower, rows_seven)
    cols_lower = raise_matrix(phi_lower, cols_seven)
    fine = jnp.einsum("kcrq,tr->kctq", patterns, rows_lower, precision=HI)
    fine = jnp.einsum("kctq,pq->kctp", fine, cols_lower, precision=HI)
    child_cos, child_sin = phases(
        codes, shift_scale[0], iota(rows_six), iota(cols_six), rows_six, cols_six
    )
    middle = jnp.sum(rotate(fine, child_cos, child_sin) * used[:, None, None, None], axis=0)

    pick_rows = halo_picker(n_samp, block_rows_six, halo_rows, rows_six)
    pick_cols = halo_picker(n_leaf, block_cols_six, halo_cols, cols_six)
    sent = jnp.einsum("crq,lkq->lcrk", middle, pick_cols, precision=HI)
    sent = jnp.einsum("lcrk,sir->lscik", sent, pick_rows, precision=HI)
    sent = sent.reshape(n_leaf * n_samp, parts, halo_rows, halo_cols)
    arrived = lax.all_to_all(sent, ("leaf", "samp"), 0, 0, tiled=True)

    theta_block = lax.dynamic_slice_in_dim(theta_upper, samp * block_rows_five, block_rows_five)
    phi_block = lax.dynamic_slice_in_dim(phi_upper, leaf * block_cols_five, block_cols_five)
    rows_up = block_matrix(theta_block, halo_rows)
    cols_up = block_matrix(phi_block, halo_cols)
    kron = jnp.einsum("ti,pk->iktp", rows_up, cols_up).reshape(
        halo_rows * halo_cols, block_size
    )
    lifted = jnp.dot(
        arrived.reshape(total_six * parts, halo_rows * halo_cols), kron, precision=HI
    ).reshape(total_six, parts, block_size)
    parents = box_codes // KIDS
    octants = box_codes % KIDS
    top_cos, top_sin = phases(
        octants,
        shift_scale[1],
        samp * block_rows_five + iota(block_rows_five),
        leaf * block_cols_five + iota(block_cols_five),
        rows_five,
        cols_five,
    )
    top_cos = top_cos.reshape(total_six, block_size)
    top_sin = top_sin.reshape(total_six, block_size)
    members = (parents[None, :] == iota(total_five)[:, None]).astype(jnp.float32)
    upward = jnp.dot(
        members,
        rotate(lifted, top_cos, top_sin).reshape(total_six, parts * block_size),
        precision=HI,
    ).reshape(total_five, parts, block_size)

    operators = translators.reshape(translators.shape[0], 2, block_size)
    sources = far_lists.reshape(-1)
    valid = (sources >= 0).astype(jnp.float32)
    picked = jnp.take(upward, jnp.maximum(sources, 0), axis=0, mode="clip")
    picked = picked * valid[:, None, None]
    chosen = jnp.take(operators, far_kinds.reshape(-1), axis=0, mode="clip")
    downward = (
        rotate(picked, chosen[:, 0], chosen[:, 1])
        .reshape(total_five, -1, parts, block_size)
        .sum(axis=1)
    )

    split = rotate(jnp.take(downward, parents, axis=0, mode="clip"), top_cos, -top_sin)
    shares = jnp.dot(
        split.reshape(total_six * parts, block_size), kron.T, precision=HI
    ).reshape(total_six, parts, halo_rows, halo_cols)
    returned = lax.all_to_all(shares, ("leaf", "samp"), 0, 0, tiled=True)
    returned = returned.reshape(n_leaf, n_samp, parts, halo_rows, halo_cols)
    mid_down = jnp.einsum("lscik,lkq->sciq", returned, pick_cols, precision=HI)
    mid_down = jnp.einsum("sciq,sir->crq", mid_down, pick_rows, precision=HI)

    spread = rotate(
        jnp.broadcast_to(mid_down, (slots,) + mid_down.shape), child_cos, -child_sin
    )
    incoming = jnp.einsum("kctq,tr->kcrq", spread, rows_lower, precision=HI)
    incoming = jnp.einsum("kcrp,pq->kcrq", incoming, cols_lower, precision=HI)
    return incoming * used[:, None, None, None]


def solution(mesh):
    placed = (
        P(("leaf", "samp"), None, None, None),
        P(("leaf", "samp")),
        P(),
        P(),
        P(),
        P(),
        P(),
        P(),
        P(),
        P(),
        P(None, None, "samp", "leaf"),
    )
    return jax.shard_map(
        body,
        mesh=mesh,
        in_specs=placed,
        out_specs=P(("leaf", "samp"), None, None, None),
        check_vma=False,
    )
```

```python
import math

import jax
import jax.numpy as jnp
from jax import lax
from jax.sharding import PartitionSpec as P

KIDS = 8
HI = lax.Precision.HIGHEST


def iota(n):
    return lax.optimization_barrier(jnp.arange(n, dtype=jnp.int32))


def raise_matrix(weights, width):
    count = weights.shape[0]
    rows = iota(count)
    columns = iota(width)
    matrix = jnp.zeros((count, width), jnp.float32)
    for stencil in range(weights.shape[1]):
        source = (rows // 2 + stencil - 1) % width
        hits = (source[:, None] == columns[None, :]).astype(jnp.float32)
        matrix = matrix + hits * weights[:, stencil][:, None]
    return matrix


def block_matrix(weights, halo):
    count = weights.shape[0]
    rows = iota(count)
    columns = iota(halo)
    matrix = jnp.zeros((count, halo), jnp.float32)
    for stencil in range(weights.shape[1]):
        hits = ((rows // 2 + stencil)[:, None] == columns[None, :]).astype(jnp.float32)
        matrix = matrix + hits * weights[:, stencil][:, None]
    return matrix


def halo_picker(blocks, block, halo, width):
    b = iota(blocks)
    i = iota(halo)
    r = iota(width)
    place = (b[:, None] * block - 1 + i[None, :]) % width
    return (place[:, :, None] == r[None, None, :]).astype(jnp.float32)


def kron_matrix(theta_block, phi_block, halo_rows, halo_cols):
    rows_five, cols_five = theta_block.shape[0], phi_block.shape[0]
    a = iota(halo_rows * halo_cols)
    b = iota(rows_five * cols_five)
    i, k = a // halo_cols, a % halo_cols
    t, p = b // cols_five, b % cols_five
    theta_rep = jnp.repeat(theta_block, cols_five, axis=0)
    phi_rep = jnp.tile(phi_block, (rows_five, 1))
    along_theta = jnp.zeros((a.shape[0], b.shape[0]), jnp.float32)
    along_phi = jnp.zeros((a.shape[0], b.shape[0]), jnp.float32)
    for stencil in range(theta_block.shape[1]):
        hit_t = (i[:, None] == (t // 2 + stencil)[None, :]).astype(jnp.float32)
        along_theta = along_theta + hit_t * theta_rep[:, stencil][None, :]
        hit_p = (k[:, None] == (p // 2 + stencil)[None, :]).astype(jnp.float32)
        along_phi = along_phi + hit_p * phi_rep[:, stencil][None, :]
    return along_theta * along_phi


def turn(field, cosine, sine):
    re0, im0, re1, im1 = field[0], field[1], field[2], field[3]
    return jnp.stack(
        [
            re0 * cosine - im0 * sine,
            re0 * sine + im0 * cosine,
            re1 * cosine - im1 * sine,
            re1 * sine + im1 * cosine,
        ]
    )


def phases(codes, kappa, theta_index, phi_index, theta_count, phi_count):
    theta = math.pi * (theta_index.astype(jnp.float32) + 0.5) / theta_count
    azimuth = 2.0 * math.pi * phi_index.astype(jnp.float32) / phi_count
    sign_x = (codes % 2).astype(jnp.float32) * 2.0 - 1.0
    sign_y = (codes // 2 % 2).astype(jnp.float32) * 2.0 - 1.0
    sign_z = (codes // 4 % 2).astype(jnp.float32) * 2.0 - 1.0
    sines = jnp.sin(theta)[:, None]
    along_x = sines * jnp.cos(azimuth)[None, :]
    along_y = sines * jnp.sin(azimuth)[None, :]
    along_z = jnp.cos(theta)[:, None] + 0.0 * azimuth[None, :]
    angle = kappa * (
        sign_x[:, None, None] * along_x
        + sign_y[:, None, None] * along_y
        + sign_z[:, None, None] * along_z
    )
    return (jnp.cos(angle), jnp.sin(angle))


def rotate(field, cosine, sine):
    count = field.shape[0]
    rest = field.shape[2:]
    grouped = field.reshape((count, 2, 2) + rest)
    real_part = grouped[:, :, 0]
    imag_part = grouped[:, :, 1]
    cosine = cosine[:, None]
    sine = sine[:, None]
    turned = jnp.stack(
        [real_part * cosine - imag_part * sine, real_part * sine + imag_part * cosine], axis=2
    )
    return turned.reshape(field.shape)


def body(
    patterns,
    child_code,
    box_codes,
    shift_scale,
    theta_lower,
    phi_lower,
    theta_upper,
    phi_upper,
    far_lists,
    far_kinds,
    translators,
):
    slots, parts, rows_seven, cols_seven = patterns.shape
    rows_six, cols_six = 2 * rows_seven, 2 * cols_seven
    rows_five, cols_five = 4 * rows_seven, 4 * cols_seven
    n_samp = lax.axis_size("samp")
    n_leaf = lax.axis_size("leaf")
    samp = lax.axis_index("samp")
    leaf = lax.axis_index("leaf")
    block_rows_six = rows_six // n_samp
    block_cols_six = cols_six // n_leaf
    block_rows_five = 2 * block_rows_six
    block_cols_five = 2 * block_cols_six
    halo_rows = block_rows_six + 3
    halo_cols = block_cols_six + 3
    total_six = box_codes.shape[0]
    total_five = far_lists.shape[0]
    block_size = block_rows_five * block_cols_five

    used = (child_code >= 0).astype(jnp.float32)
    codes = jnp.maximum(child_code, 0)
    rows_lower = raise_matrix(theta_lower, rows_seven)
    cols_lower = raise_matrix(phi_lower, cols_seven)
    fine = jnp.einsum("kcrq,tr->kctq", patterns, rows_lower, precision=HI)
    fine = jnp.einsum("kctq,pq->kctp", fine, cols_lower, precision=HI)
    child_cos, child_sin = phases(
        codes, shift_scale[0], iota(rows_six), iota(cols_six), rows_six, cols_six
    )
    middle = jnp.sum(rotate(fine, child_cos, child_sin) * used[:, None, None, None], axis=0)

    pick_rows = halo_picker(n_samp, block_rows_six, halo_rows, rows_six)
    pick_cols = halo_picker(n_leaf, block_cols_six, halo_cols, cols_six)
    sent = jnp.einsum("crq,sir->csiq", middle, pick_rows, precision=HI)
    sent = jnp.einsum("csiq,lkq->lscik", sent, pick_cols, precision=HI)
    sent = sent.reshape(n_leaf * n_samp, parts, halo_rows, halo_cols)
    arrived = lax.all_to_all(sent, ("leaf", "samp"), 0, 0, tiled=True)

    theta_block = lax.dynamic_slice_in_dim(theta_upper, samp * block_rows_five, block_rows_five)
    phi_block = lax.dynamic_slice_in_dim(phi_upper, leaf * block_cols_five, block_cols_five)
    kron = kron_matrix(theta_block, phi_block, halo_rows, halo_cols)
    gathered = arrived.reshape(total_six, parts, halo_rows * halo_cols).transpose(1, 0, 2)
    lifted = jnp.einsum("cbn,nx->cbx", gathered, kron, precision=HI)
    parents = box_codes // KIDS
    octants = box_codes % KIDS
    top_cos, top_sin = phases(
        octants,
        shift_scale[1],
        samp * block_rows_five + iota(block_rows_five),
        leaf * block_cols_five + iota(block_cols_five),
        rows_five,
        cols_five,
    )
    top_cos = top_cos.reshape(total_six, block_size)
    top_sin = top_sin.reshape(total_six, block_size)
    members = (parents[None, :] == iota(total_five)[:, None]).astype(jnp.float32)
    upward = jnp.einsum(
        "qb,cbx->cqx", members, turn(lifted, top_cos, top_sin), precision=HI
    )

    entries = far_lists.reshape(-1)
    pick_source = (entries[:, None] == iota(total_five)[None, :]).astype(jnp.float32)
    kinds = far_kinds.reshape(-1)
    pick_kind = (kinds[:, None] == iota(translators.shape[0])[None, :]).astype(jnp.float32)
    operators = translators.reshape(translators.shape[0], 2, block_size)
    chosen = jnp.einsum("nk,krx->rnx", pick_kind, operators, precision=HI)
    picked = jnp.einsum("nq,cqx->cnx", pick_source, upward, precision=HI)
    downward = turn(picked, chosen[0], chosen[1])
    downward = downward.reshape(parts, total_five, -1, block_size).sum(axis=2)

    split = jnp.einsum("qb,cqx->cbx", members, downward, precision=HI)
    split = turn(split, top_cos, -top_sin)
    shares = jnp.einsum("cbx,nx->bcn", split, kron, precision=HI)
    shares = shares.reshape(total_six, parts, halo_rows, halo_cols)
    returned = lax.all_to_all(shares, ("leaf", "samp"), 0, 0, tiled=True)
    returned = returned.reshape(n_leaf, n_samp, parts, halo_rows, halo_cols)
    mid_down = jnp.einsum("lscik,lkq->csiq", returned, pick_cols, precision=HI)
    mid_down = jnp.einsum("csiq,sir->crq", mid_down, pick_rows, precision=HI)

    spread = rotate(
        jnp.broadcast_to(mid_down, (slots,) + mid_down.shape), child_cos, -child_sin
    )
    incoming = jnp.einsum("kctq,tr->kcrq", spread, rows_lower, precision=HI)
    incoming = jnp.einsum("kcrp,pq->kcrq", incoming, cols_lower, precision=HI)
    return incoming * used[:, None, None, None]


def solution(mesh):
    placed = (
        P(("leaf", "samp"), None, None, None),
        P(("leaf", "samp")),
        P(),
        P(),
        P(),
        P(),
        P(),
        P(),
        P(),
        P(),
        P(None, None, "samp", "leaf"),
    )
    return jax.shard_map(
        body,
        mesh=mesh,
        in_specs=placed,
        out_specs=P(("leaf", "samp"), None, None, None),
        check_vma=False,
    )
```

```python
import math

import jax
import jax.numpy as jnp
from jax import lax
from jax.sharding import PartitionSpec as P

KIDS = 8
HI = lax.Precision.HIGHEST


def iota(n):
    return lax.optimization_barrier(jnp.arange(n, dtype=jnp.int32))


def raise_matrix(weights, width):
    count = weights.shape[0]
    rows = iota(count)
    columns = iota(width)
    matrix = jnp.zeros((count, width), jnp.float32)
    for stencil in range(weights.shape[1]):
        source = (rows // 2 + stencil - 1) % width
        hits = (source[:, None] == columns[None, :]).astype(jnp.float32)
        matrix = matrix + hits * weights[:, stencil][:, None]
    return matrix


def block_matrix(weights, halo):
    count = weights.shape[0]
    rows = iota(count)
    columns = iota(halo)
    matrix = jnp.zeros((count, halo), jnp.float32)
    for stencil in range(weights.shape[1]):
        hits = ((rows // 2 + stencil)[:, None] == columns[None, :]).astype(jnp.float32)
        matrix = matrix + hits * weights[:, stencil][:, None]
    return matrix


def halo_picker(blocks, block, halo, width):
    b = iota(blocks)
    i = iota(halo)
    r = iota(width)
    place = (b[:, None] * block - 1 + i[None, :]) % width
    return (place[:, :, None] == r[None, None, :]).astype(jnp.float32)


def kron_matrix(theta_block, phi_block, halo_rows, halo_cols):
    rows_five, cols_five = theta_block.shape[0], phi_block.shape[0]
    a = iota(halo_rows * halo_cols)
    b = iota(rows_five * cols_five)
    i, k = a // halo_cols, a % halo_cols
    t, p = b // cols_five, b % cols_five
    theta_rep = jnp.repeat(theta_block, cols_five, axis=0)
    phi_rep = jnp.tile(phi_block, (rows_five, 1))
    along_theta = jnp.zeros((a.shape[0], b.shape[0]), jnp.float32)
    along_phi = jnp.zeros((a.shape[0], b.shape[0]), jnp.float32)
    for stencil in range(theta_block.shape[1]):
        hit_t = (i[:, None] == (t // 2 + stencil)[None, :]).astype(jnp.float32)
        along_theta = along_theta + hit_t * theta_rep[:, stencil][None, :]
        hit_p = (k[:, None] == (p // 2 + stencil)[None, :]).astype(jnp.float32)
        along_phi = along_phi + hit_p * phi_rep[:, stencil][None, :]
    return along_theta * along_phi


def turn(field, cosine, sine):
    turned = []
    for pol in range(field.shape[0] // 2):
        re, im = field[2 * pol], field[2 * pol + 1]
        turned += [re * cosine - im * sine, re * sine + im * cosine]
    return jnp.stack(turned)


def phases(codes, kappa, theta_index, phi_index, theta_count, phi_count):
    theta = math.pi * (theta_index.astype(jnp.float32) + 0.5) / theta_count
    azimuth = 2.0 * math.pi * phi_index.astype(jnp.float32) / phi_count
    sign_x = (codes % 2).astype(jnp.float32) * 2.0 - 1.0
    sign_y = (codes // 2 % 2).astype(jnp.float32) * 2.0 - 1.0
    sign_z = (codes // 4 % 2).astype(jnp.float32) * 2.0 - 1.0
    sines = jnp.sin(theta)[:, None]
    along_x = sines * jnp.cos(azimuth)[None, :]
    along_y = sines * jnp.sin(azimuth)[None, :]
    along_z = jnp.cos(theta)[:, None] + 0.0 * azimuth[None, :]
    angle = kappa * (
        sign_x[:, None, None] * along_x
        + sign_y[:, None, None] * along_y
        + sign_z[:, None, None] * along_z
    )
    return (jnp.cos(angle), jnp.sin(angle))


def rotate(field, cosine, sine):
    count = field.shape[0]
    rest = field.shape[2:]
    grouped = field.reshape((count, field.shape[1] // 2, 2) + rest)
    real_part = grouped[:, :, 0]
    imag_part = grouped[:, :, 1]
    cosine = cosine[:, None]
    sine = sine[:, None]
    turned = jnp.stack(
        [real_part * cosine - imag_part * sine, real_part * sine + imag_part * cosine], axis=2
    )
    return turned.reshape(field.shape)


def body(
    patterns,
    child_code,
    box_codes,
    shift_scale,
    theta_lower,
    phi_lower,
    theta_upper,
    phi_upper,
    far_lists,
    far_kinds,
    translators,
):
    slots, parts, rows_seven, cols_seven = patterns.shape
    rows_six, cols_six = 2 * rows_seven, 2 * cols_seven
    rows_five, cols_five = 4 * rows_seven, 4 * cols_seven
    n_samp = lax.axis_size("samp")
    n_leaf = lax.axis_size("leaf")
    samp = lax.axis_index("samp")
    leaf = lax.axis_index("leaf")
    block_rows_six = rows_six // n_samp
    block_cols_six = cols_six // n_leaf
    block_rows_five = 2 * block_rows_six
    block_cols_five = 2 * block_cols_six
    halo_rows = block_rows_six + 3
    halo_cols = block_cols_six + 3
    total_six = box_codes.shape[0]
    total_five = far_lists.shape[0]
    block_size = block_rows_five * block_cols_five

    used = (child_code >= 0).astype(jnp.float32)
    codes = jnp.maximum(child_code, 0)
    rows_lower = raise_matrix(theta_lower, rows_seven)
    cols_lower = raise_matrix(phi_lower, cols_seven)
    fine = jnp.einsum("kcrq,tr->kctq", patterns, rows_lower, precision=HI)
    fine = jnp.einsum("kctq,pq->kctp", fine, cols_lower, precision=HI)
    child_cos, child_sin = phases(
        codes, shift_scale[0], iota(rows_six), iota(cols_six), rows_six, cols_six
    )
    pick_rows = halo_picker(n_samp, block_rows_six, halo_rows, rows_six)
    pick_cols = halo_picker(n_leaf, block_cols_six, halo_cols, cols_six)
    theta_block = lax.dynamic_slice_in_dim(theta_upper, samp * block_rows_five, block_rows_five)
    phi_block = lax.dynamic_slice_in_dim(phi_upper, leaf * block_cols_five, block_cols_five)
    kron = kron_matrix(theta_block, phi_block, halo_rows, halo_cols)
    parents = box_codes // KIDS
    octants = box_codes % KIDS
    top_cos, top_sin = phases(
        octants,
        shift_scale[1],
        samp * block_rows_five + iota(block_rows_five),
        leaf * block_cols_five + iota(block_cols_five),
        rows_five,
        cols_five,
    )
    top_cos = top_cos.reshape(total_six, block_size)
    top_sin = top_sin.reshape(total_six, block_size)
    members = (parents[None, :] == iota(total_five)[:, None]).astype(jnp.float32)
    entries = far_lists.reshape(-1)
    pick_source = (entries[:, None] == iota(total_five)[None, :]).astype(jnp.float32)
    kinds = far_kinds.reshape(-1)
    pick_kind = (kinds[:, None] == iota(translators.shape[0])[None, :]).astype(jnp.float32)
    operators = translators.reshape(translators.shape[0], 2, block_size)
    chosen = jnp.einsum("nk,krx->rnx", pick_kind, operators, precision=HI)

    def polarization(fine_part):
        comps = fine_part.shape[1]
        middle = jnp.sum(
            rotate(fine_part, child_cos, child_sin) * used[:, None, None, None], axis=0
        )
        sent = jnp.einsum("crq,sir->csiq", middle, pick_rows, precision=HI)
        sent = jnp.einsum("csiq,lkq->lscik", sent, pick_cols, precision=HI)
        sent = sent.reshape(n_leaf * n_samp, comps, halo_rows, halo_cols)
        arrived = lax.all_to_all(sent, ("leaf", "samp"), 0, 0, tiled=True)

        gathered = arrived.reshape(total_six, comps, halo_rows * halo_cols).transpose(1, 0, 2)
        lifted = jnp.einsum("cbn,nx->cbx", gathered, kron, precision=HI)
        upward = jnp.einsum(
            "qb,cbx->cqx", members, turn(lifted, top_cos, top_sin), precision=HI
        )

        picked = jnp.einsum("nq,cqx->cnx", pick_source, upward, precision=HI)
        downward = turn(picked, chosen[0], chosen[1])
        downward = downward.reshape(comps, total_five, -1, block_size).sum(axis=2)

        split = jnp.einsum("qb,cqx->cbx", members, downward, precision=HI)
        split = turn(split, top_cos, -top_sin)
        shares = jnp.einsum("cbx,nx->bcn", split, kron, precision=HI)
        shares = shares.reshape(total_six, comps, halo_rows, halo_cols)
        returned = lax.all_to_all(shares, ("leaf", "samp"), 0, 0, tiled=True)
        returned = returned.reshape(n_leaf, n_samp, comps, halo_rows, halo_cols)
        mid_down = jnp.einsum("lscik,lkq->csiq", returned, pick_cols, precision=HI)
        mid_down = jnp.einsum("csiq,sir->crq", mid_down, pick_rows, precision=HI)

        spread = rotate(
            jnp.broadcast_to(mid_down, (slots,) + mid_down.shape), child_cos, -child_sin
        )
        incoming = jnp.einsum("kctq,tr->kcrq", spread, rows_lower, precision=HI)
        incoming = jnp.einsum("kcrp,pq->kcrq", incoming, cols_lower, precision=HI)
        return incoming * used[:, None, None, None]

    halves = [polarization(fine[:, 2 * pol : 2 * pol + 2]) for pol in range(parts // 2)]
    return jnp.concatenate(halves, axis=1)


def solution(mesh):
    placed = (
        P(("leaf", "samp"), None, None, None),
        P(("leaf", "samp")),
        P(),
        P(),
        P(),
        P(),
        P(),
        P(),
        P(),
        P(),
        P(None, None, "samp", "leaf"),
    )
    return jax.shard_map(
        body,
        mesh=mesh,
        in_specs=placed,
        out_specs=P(("leaf", "samp"), None, None, None),
        check_vma=False,
    )
```

```python
import math

import jax
import jax.numpy as jnp
from jax import lax
from jax.sharding import PartitionSpec as P

KIDS = 8
HI = lax.Precision.HIGH


def iota(n):
    return lax.optimization_barrier(jnp.arange(n, dtype=jnp.int32))


def raise_matrix(weights, width):
    count = weights.shape[0]
    rows = iota(count)
    columns = iota(width)
    matrix = jnp.zeros((count, width), jnp.float32)
    for stencil in range(weights.shape[1]):
        source = (rows // 2 + stencil - 1) % width
        hits = (source[:, None] == columns[None, :]).astype(jnp.float32)
        matrix = matrix + hits * weights[:, stencil][:, None]
    return matrix


def block_matrix(weights, halo):
    count = weights.shape[0]
    rows = iota(count)
    columns = iota(halo)
    matrix = jnp.zeros((count, halo), jnp.float32)
    for stencil in range(weights.shape[1]):
        hits = ((rows // 2 + stencil)[:, None] == columns[None, :]).astype(jnp.float32)
        matrix = matrix + hits * weights[:, stencil][:, None]
    return matrix


def halo_picker(blocks, block, halo, width):
    b = iota(blocks)
    i = iota(halo)
    r = iota(width)
    place = (b[:, None] * block - 1 + i[None, :]) % width
    return (place[:, :, None] == r[None, None, :]).astype(jnp.float32)


def kron_matrix(theta_block, phi_block, halo_rows, halo_cols):
    rows_five, cols_five = theta_block.shape[0], phi_block.shape[0]
    a = iota(halo_rows * halo_cols)
    b = iota(rows_five * cols_five)
    i, k = a // halo_cols, a % halo_cols
    t, p = b // cols_five, b % cols_five
    theta_rep = jnp.repeat(theta_block, cols_five, axis=0)
    phi_rep = jnp.tile(phi_block, (rows_five, 1))
    along_theta = jnp.zeros((a.shape[0], b.shape[0]), jnp.float32)
    along_phi = jnp.zeros((a.shape[0], b.shape[0]), jnp.float32)
    for stencil in range(theta_block.shape[1]):
        hit_t = (i[:, None] == (t // 2 + stencil)[None, :]).astype(jnp.float32)
        along_theta = along_theta + hit_t * theta_rep[:, stencil][None, :]
        hit_p = (k[:, None] == (p // 2 + stencil)[None, :]).astype(jnp.float32)
        along_phi = along_phi + hit_p * phi_rep[:, stencil][None, :]
    return along_theta * along_phi


def turn(field, cosine, sine):
    turned = []
    for pol in range(field.shape[0] // 2):
        re, im = field[2 * pol], field[2 * pol + 1]
        turned += [re * cosine - im * sine, re * sine + im * cosine]
    return jnp.stack(turned)


def phases(codes, kappa, theta_index, phi_index, theta_count, phi_count):
    theta = math.pi * (theta_index.astype(jnp.float32) + 0.5) / theta_count
    azimuth = 2.0 * math.pi * phi_index.astype(jnp.float32) / phi_count
    sign_x = ((codes % 2).astype(jnp.float32) * 2.0 - 1.0)[:, None, None]
    sign_y = ((codes // 2 % 2).astype(jnp.float32) * 2.0 - 1.0)[:, None, None]
    sign_z = ((codes // 4 % 2).astype(jnp.float32) * 2.0 - 1.0)[:, None, None]
    sines = jnp.sin(theta)[:, None]
    along_x = kappa * (sines * jnp.cos(azimuth)[None, :])
    along_y = kappa * (sines * jnp.sin(azimuth)[None, :])
    along_z = kappa * jnp.cos(theta)[:, None]
    cos_x, sin_x = jnp.cos(along_x), jnp.sin(along_x)
    cos_y, sin_y = jnp.cos(along_y), jnp.sin(along_y)
    cos_z, sin_z = jnp.cos(along_z), jnp.sin(along_z)
    plane_re = cos_x * cos_y - (sign_x * sign_y) * (sin_x * sin_y)
    plane_im = sign_x * (sin_x * cos_y) + sign_y * (cos_x * sin_y)
    signed_z = sign_z * sin_z
    return (plane_re * cos_z - plane_im * signed_z, plane_re * signed_z + plane_im * cos_z)


def rotate(field, cosine, sine):
    count = field.shape[0]
    rest = field.shape[2:]
    grouped = field.reshape((count, field.shape[1] // 2, 2) + rest)
    real_part = grouped[:, :, 0]
    imag_part = grouped[:, :, 1]
    cosine = cosine[:, None]
    sine = sine[:, None]
    turned = jnp.stack(
        [real_part * cosine - imag_part * sine, real_part * sine + imag_part * cosine], axis=2
    )
    return turned.reshape(field.shape)


def body(
    patterns,
    child_code,
    box_codes,
    shift_scale,
    theta_lower,
    phi_lower,
    theta_upper,
    phi_upper,
    far_lists,
    far_kinds,
    translators,
):
    slots, parts, rows_seven, cols_seven = patterns.shape
    rows_six, cols_six = 2 * rows_seven, 2 * cols_seven
    rows_five, cols_five = 4 * rows_seven, 4 * cols_seven
    n_samp = lax.axis_size("samp")
    n_leaf = lax.axis_size("leaf")
    samp = lax.axis_index("samp")
    leaf = lax.axis_index("leaf")
    block_rows_six = rows_six // n_samp
    block_cols_six = cols_six // n_leaf
    block_rows_five = 2 * block_rows_six
    block_cols_five = 2 * block_cols_six
    halo_rows = block_rows_six + 3
    halo_cols = block_cols_six + 3
    total_six = box_codes.shape[0]
    total_five = far_lists.shape[0]
    block_size = block_rows_five * block_cols_five

    used = (child_code >= 0).astype(jnp.float32)
    codes = jnp.maximum(child_code, 0)
    rows_lower = raise_matrix(theta_lower, rows_seven)
    cols_lower = raise_matrix(phi_lower, cols_seven)
    fine = jnp.einsum("kcrq,tr->kctq", patterns, rows_lower, precision=HI)
    fine = jnp.einsum("kctq,pq->kctp", fine, cols_lower, precision=HI)
    child_cos, child_sin = phases(
        codes, shift_scale[0], iota(rows_six), iota(cols_six), rows_six, cols_six
    )
    pick_rows = halo_picker(n_samp, block_rows_six, halo_rows, rows_six)
    pick_cols = halo_picker(n_leaf, block_cols_six, halo_cols, cols_six)
    theta_block = lax.dynamic_slice_in_dim(theta_upper, samp * block_rows_five, block_rows_five)
    phi_block = lax.dynamic_slice_in_dim(phi_upper, leaf * block_cols_five, block_cols_five)
    kron = kron_matrix(theta_block, phi_block, halo_rows, halo_cols)
    parents = box_codes // KIDS
    octants = box_codes % KIDS
    top_cos, top_sin = phases(
        octants,
        shift_scale[1],
        samp * block_rows_five + iota(block_rows_five),
        leaf * block_cols_five + iota(block_cols_five),
        rows_five,
        cols_five,
    )
    top_cos = top_cos.reshape(total_six, block_size)
    top_sin = top_sin.reshape(total_six, block_size)
    members = (parents[None, :] == iota(total_five)[:, None]).astype(jnp.float32)
    entries = far_lists.reshape(-1)
    pick_source = (entries[:, None] == iota(total_five)[None, :]).astype(jnp.float32)
    kinds = far_kinds.reshape(-1)
    pick_kind = (kinds[:, None] == iota(translators.shape[0])[None, :]).astype(jnp.float32)
    operators = translators.reshape(translators.shape[0], 2, block_size)
    chosen = jnp.einsum("nk,krx->rnx", pick_kind, operators, precision=HI)

    def polarization(fine_part):
        comps = fine_part.shape[1]
        middle = jnp.sum(
            rotate(fine_part, child_cos, child_sin) * used[:, None, None, None], axis=0
        )
        sent = jnp.einsum("crq,sir->csiq", middle, pick_rows, precision=HI)
        sent = jnp.einsum("csiq,lkq->lscik", sent, pick_cols, precision=HI)
        sent = sent.reshape(n_leaf * n_samp, comps, halo_rows, halo_cols)
        arrived = lax.all_to_all(sent, ("leaf", "samp"), 0, 0, tiled=True)

        gathered = arrived.reshape(total_six, comps, halo_rows * halo_cols).transpose(1, 0, 2)
        lifted = jnp.einsum("cbn,nx->cbx", gathered, kron, precision=HI)
        upward = jnp.einsum(
            "qb,cbx->cqx", members, turn(lifted, top_cos, top_sin), precision=HI
        )

        picked = jnp.einsum("nq,cqx->cnx", pick_source, upward, precision=HI)
        downward = turn(picked, chosen[0], chosen[1])
        downward = downward.reshape(comps, total_five, -1, block_size).sum(axis=2)

        split = jnp.einsum("qb,cqx->cbx", members, downward, precision=HI)
        split = turn(split, top_cos, -top_sin)
        shares = jnp.einsum("cbx,nx->bcn", split, kron, precision=HI)
        shares = shares.reshape(total_six, comps, halo_rows, halo_cols)
        returned = lax.all_to_all(shares, ("leaf", "samp"), 0, 0, tiled=True)
        returned = returned.reshape(n_leaf, n_samp, comps, halo_rows, halo_cols)
        mid_down = jnp.einsum("lscik,lkq->csiq", returned, pick_cols, precision=HI)
        mid_down = jnp.einsum("csiq,sir->crq", mid_down, pick_rows, precision=HI)

        spread = rotate(
            jnp.broadcast_to(mid_down, (slots,) + mid_down.shape), child_cos, -child_sin
        )
        incoming = jnp.einsum("kctq,tr->kcrq", spread, rows_lower, precision=HI)
        incoming = jnp.einsum("kcrp,pq->kcrq", incoming, cols_lower, precision=HI)
        return incoming * used[:, None, None, None]

    halves = [polarization(fine[:, 2 * pol : 2 * pol + 2]) for pol in range(parts // 2)]
    return jnp.concatenate(halves, axis=1)


def solution(mesh):
    placed = (
        P(("leaf", "samp"), None, None, None),
        P(("leaf", "samp")),
        P(),
        P(),
        P(),
        P(),
        P(),
        P(),
        P(),
        P(),
        P(None, None, "samp", "leaf"),
    )
    return jax.shard_map(
        body,
        mesh=mesh,
        in_specs=placed,
        out_specs=P(("leaf", "samp"), None, None, None),
        check_vma=False,
    )
```

```python
import math

import jax
import jax.numpy as jnp
from jax import lax
from jax.sharding import PartitionSpec as P

KIDS = 8
HI = lax.Precision.HIGH


def iota(n):
    return lax.optimization_barrier(jnp.arange(n, dtype=jnp.int32))


def raise_matrix(weights, width):
    count = weights.shape[0]
    rows = iota(count)
    columns = iota(width)
    matrix = jnp.zeros((count, width), jnp.float32)
    for stencil in range(weights.shape[1]):
        source = (rows // 2 + stencil - 1) % width
        hits = (source[:, None] == columns[None, :]).astype(jnp.float32)
        matrix = matrix + hits * weights[:, stencil][:, None]
    return matrix


def block_matrix(weights, halo):
    count = weights.shape[0]
    rows = iota(count)
    columns = iota(halo)
    matrix = jnp.zeros((count, halo), jnp.float32)
    for stencil in range(weights.shape[1]):
        hits = ((rows // 2 + stencil)[:, None] == columns[None, :]).astype(jnp.float32)
        matrix = matrix + hits * weights[:, stencil][:, None]
    return matrix


def halo_picker(blocks, block, halo, width):
    b = iota(blocks)
    i = iota(halo)
    r = iota(width)
    place = (b[:, None] * block - 1 + i[None, :]) % width
    return (place[:, :, None] == r[None, None, :]).astype(jnp.float32)


def kron_matrix(theta_block, phi_block, halo_rows, halo_cols):
    rows_five, cols_five = theta_block.shape[0], phi_block.shape[0]
    a = iota(halo_rows * halo_cols)
    b = iota(rows_five * cols_five)
    i, k = a // halo_cols, a % halo_cols
    t, p = b // cols_five, b % cols_five
    theta_rep = jnp.repeat(theta_block, cols_five, axis=0)
    phi_rep = jnp.tile(phi_block, (rows_five, 1))
    along_theta = jnp.zeros((a.shape[0], b.shape[0]), jnp.float32)
    along_phi = jnp.zeros((a.shape[0], b.shape[0]), jnp.float32)
    for stencil in range(theta_block.shape[1]):
        hit_t = (i[:, None] == (t // 2 + stencil)[None, :]).astype(jnp.float32)
        along_theta = along_theta + hit_t * theta_rep[:, stencil][None, :]
        hit_p = (k[:, None] == (p // 2 + stencil)[None, :]).astype(jnp.float32)
        along_phi = along_phi + hit_p * phi_rep[:, stencil][None, :]
    return along_theta * along_phi


def turn(field, cosine, sine):
    turned = []
    for pol in range(field.shape[0] // 2):
        re, im = field[2 * pol], field[2 * pol + 1]
        turned += [re * cosine - im * sine, re * sine + im * cosine]
    return jnp.stack(turned)


def phases(codes, kappa, theta_index, phi_index, theta_count, phi_count):
    theta = math.pi * (theta_index.astype(jnp.float32) + 0.5) / theta_count
    azimuth = 2.0 * math.pi * phi_index.astype(jnp.float32) / phi_count
    sign_x = ((codes % 2).astype(jnp.float32) * 2.0 - 1.0)[:, None, None]
    sign_y = ((codes // 2 % 2).astype(jnp.float32) * 2.0 - 1.0)[:, None, None]
    sign_z = ((codes // 4 % 2).astype(jnp.float32) * 2.0 - 1.0)[:, None, None]
    sines = jnp.sin(theta)[:, None]
    along_x = kappa * (sines * jnp.cos(azimuth)[None, :])
    along_y = kappa * (sines * jnp.sin(azimuth)[None, :])
    along_z = kappa * jnp.cos(theta)[:, None]
    cos_x, sin_x = jnp.cos(along_x), jnp.sin(along_x)
    cos_y, sin_y = jnp.cos(along_y), jnp.sin(along_y)
    cos_z, sin_z = jnp.cos(along_z), jnp.sin(along_z)
    plane_re = cos_x * cos_y - (sign_x * sign_y) * (sin_x * sin_y)
    plane_im = sign_x * (sin_x * cos_y) + sign_y * (cos_x * sin_y)
    signed_z = sign_z * sin_z
    return (plane_re * cos_z - plane_im * signed_z, plane_re * signed_z + plane_im * cos_z)


def rotate(field, cosine, sine):
    count = field.shape[0]
    rest = field.shape[2:]
    grouped = field.reshape((count, field.shape[1] // 2, 2) + rest)
    real_part = grouped[:, :, 0]
    imag_part = grouped[:, :, 1]
    cosine = cosine[:, None]
    sine = sine[:, None]
    turned = jnp.stack(
        [real_part * cosine - imag_part * sine, real_part * sine + imag_part * cosine], axis=2
    )
    return turned.reshape(field.shape)


def body(
    patterns,
    child_code,
    box_codes,
    shift_scale,
    theta_lower,
    phi_lower,
    theta_upper,
    phi_upper,
    far_lists,
    far_kinds,
    translators,
):
    slots, parts, rows_seven, cols_seven = patterns.shape
    rows_six, cols_six = 2 * rows_seven, 2 * cols_seven
    rows_five, cols_five = 4 * rows_seven, 4 * cols_seven
    n_samp = lax.axis_size("samp")
    n_leaf = lax.axis_size("leaf")
    samp = lax.axis_index("samp")
    leaf = lax.axis_index("leaf")
    block_rows_six = rows_six // n_samp
    block_cols_six = cols_six // n_leaf
    block_rows_five = 2 * block_rows_six
    block_cols_five = 2 * block_cols_six
    halo_rows = block_rows_six + 3
    halo_cols = block_cols_six + 3
    total_six = box_codes.shape[0]
    total_five = far_lists.shape[0]
    block_size = block_rows_five * block_cols_five

    used = (child_code >= 0).astype(jnp.float32)
    codes = jnp.maximum(child_code, 0)
    rows_lower = raise_matrix(theta_lower, rows_seven)
    cols_lower = raise_matrix(phi_lower, cols_seven)
    fine = jnp.einsum("kcrq,tr->kctq", patterns, rows_lower, precision=HI)
    fine = jnp.einsum("kctq,pq->kctp", fine, cols_lower, precision=HI)
    child_cos, child_sin = phases(
        codes, shift_scale[0], iota(rows_six), iota(cols_six), rows_six, cols_six
    )
    pick_rows = halo_picker(n_samp, block_rows_six, halo_rows, rows_six)
    pick_cols = halo_picker(n_leaf, block_cols_six, halo_cols, cols_six)
    theta_block = lax.dynamic_slice_in_dim(theta_upper, samp * block_rows_five, block_rows_five)
    phi_block = lax.dynamic_slice_in_dim(phi_upper, leaf * block_cols_five, block_cols_five)
    kron = kron_matrix(theta_block, phi_block, halo_rows, halo_cols)
    parents = box_codes // KIDS
    octants = box_codes % KIDS
    top_cos, top_sin = phases(
        octants,
        shift_scale[1],
        samp * block_rows_five + iota(block_rows_five),
        leaf * block_cols_five + iota(block_cols_five),
        rows_five,
        cols_five,
    )
    top_cos = top_cos.reshape(total_six, block_size)
    top_sin = top_sin.reshape(total_six, block_size)
    members = (parents[None, :] == iota(total_five)[:, None]).astype(jnp.float32)
    entries = far_lists.reshape(-1)
    pick_source = (entries[:, None] == iota(total_five)[None, :]).astype(jnp.float32)
    kinds = far_kinds.reshape(-1)
    pick_kind = (kinds[:, None] == iota(translators.shape[0])[None, :]).astype(jnp.float32)
    operators = translators.reshape(translators.shape[0], 2, block_size)
    chosen = jnp.einsum("nk,krx->rnx", pick_kind, operators, precision=HI)

    def polarization(fine_part):
        comps = fine_part.shape[1]
        middle = jnp.sum(
            rotate(fine_part, child_cos, child_sin) * used[:, None, None, None], axis=0
        )
        sent = jnp.einsum("crq,sir->csiq", middle, pick_rows, precision=HI)
        sent = jnp.einsum("csiq,lkq->lscik", sent, pick_cols, precision=HI)
        sent = sent.reshape(n_leaf * n_samp, comps * halo_rows * halo_cols)
        arrived = lax.all_to_all(sent, ("leaf", "samp"), 0, 0, tiled=True)

        gathered = arrived.reshape(total_six, comps, halo_rows * halo_cols).transpose(1, 0, 2)
        lifted = jnp.einsum("cbn,nx->cbx", gathered, kron, precision=HI)
        upward = jnp.einsum(
            "qb,cbx->cqx", members, turn(lifted, top_cos, top_sin), precision=HI
        )

        picked = jnp.einsum("nq,cqx->cnx", pick_source, upward, precision=HI)
        downward = turn(picked, chosen[0], chosen[1])
        downward = downward.reshape(comps, total_five, -1, block_size).sum(axis=2)

        split = jnp.einsum("qb,cqx->cbx", members, downward, precision=HI)
        split = turn(split, top_cos, -top_sin)
        shares = jnp.einsum("cbx,nx->bcn", split, kron, precision=HI)
        shares = shares.reshape(total_six, comps * halo_rows * halo_cols)
        returned = lax.all_to_all(shares, ("leaf", "samp"), 0, 0, tiled=True)
        returned = returned.reshape(n_leaf, n_samp, comps, halo_rows, halo_cols)
        mid_down = jnp.einsum("lscik,lkq->csiq", returned, pick_cols, precision=HI)
        mid_down = jnp.einsum("csiq,sir->crq", mid_down, pick_rows, precision=HI)

        spread = rotate(
            jnp.broadcast_to(mid_down, (slots,) + mid_down.shape), child_cos, -child_sin
        )
        incoming = jnp.einsum("kctq,tr->kcrq", spread, rows_lower, precision=HI)
        incoming = jnp.einsum("kcrp,pq->kcrq", incoming, cols_lower, precision=HI)
        return incoming * used[:, None, None, None]

    halves = [polarization(fine[:, 2 * pol : 2 * pol + 2]) for pol in range(parts // 2)]
    return jnp.concatenate(halves, axis=1)


def solution(mesh):
    placed = (
        P(("leaf", "samp"), None, None, None),
        P(("leaf", "samp")),
        P(),
        P(),
        P(),
        P(),
        P(),
        P(),
        P(),
        P(),
        P(None, None, "samp", "leaf"),
    )
    return jax.shard_map(
        body,
        mesh=mesh,
        in_specs=placed,
        out_specs=P(("leaf", "samp"), None, None, None),
        check_vma=False,
    )
```

```python
import math

import jax
import jax.numpy as jnp
from jax import lax
from jax.sharding import PartitionSpec as P

KIDS = 8
HI = lax.Precision.HIGH


def iota(n):
    return lax.optimization_barrier(jnp.arange(n, dtype=jnp.int32))


def raise_matrix(weights, width):
    count = weights.shape[0]
    rows = iota(count)
    columns = iota(width)
    matrix = jnp.zeros((count, width), jnp.float32)
    for stencil in range(weights.shape[1]):
        source = (rows // 2 + stencil - 1) % width
        hits = (source[:, None] == columns[None, :]).astype(jnp.float32)
        matrix = matrix + hits * weights[:, stencil][:, None]
    return matrix


def block_matrix(weights, halo):
    count = weights.shape[0]
    rows = iota(count)
    columns = iota(halo)
    matrix = jnp.zeros((count, halo), jnp.float32)
    for stencil in range(weights.shape[1]):
        hits = ((rows // 2 + stencil)[:, None] == columns[None, :]).astype(jnp.float32)
        matrix = matrix + hits * weights[:, stencil][:, None]
    return matrix


def halo_picker(blocks, block, halo, width):
    b = iota(blocks)
    i = iota(halo)
    r = iota(width)
    place = (b[:, None] * block - 1 + i[None, :]) % width
    return (place[:, :, None] == r[None, None, :]).astype(jnp.float32)


def kron_matrix(theta_block, phi_block, halo_rows, halo_cols):
    rows_five, cols_five = theta_block.shape[0], phi_block.shape[0]
    a = iota(halo_rows * halo_cols)
    b = iota(rows_five * cols_five)
    i, k = a // halo_cols, a % halo_cols
    t, p = b // cols_five, b % cols_five
    theta_rep = jnp.repeat(theta_block, cols_five, axis=0)
    phi_rep = jnp.tile(phi_block, (rows_five, 1))
    along_theta = jnp.zeros((a.shape[0], b.shape[0]), jnp.float32)
    along_phi = jnp.zeros((a.shape[0], b.shape[0]), jnp.float32)
    for stencil in range(theta_block.shape[1]):
        hit_t = (i[:, None] == (t // 2 + stencil)[None, :]).astype(jnp.float32)
        along_theta = along_theta + hit_t * theta_rep[:, stencil][None, :]
        hit_p = (k[:, None] == (p // 2 + stencil)[None, :]).astype(jnp.float32)
        along_phi = along_phi + hit_p * phi_rep[:, stencil][None, :]
    return along_theta * along_phi


def turn(field, cosine, sine):
    turned = []
    for pol in range(field.shape[0] // 2):
        re, im = field[2 * pol], field[2 * pol + 1]
        turned += [re * cosine - im * sine, re * sine + im * cosine]
    return jnp.stack(turned)


def phases(codes, kappa, theta_index, phi_index, theta_count, phi_count):
    theta = math.pi * (theta_index.astype(jnp.float32) + 0.5) / theta_count
    azimuth = 2.0 * math.pi * phi_index.astype(jnp.float32) / phi_count
    sign_x = ((codes % 2).astype(jnp.float32) * 2.0 - 1.0)[:, None, None]
    sign_y = ((codes // 2 % 2).astype(jnp.float32) * 2.0 - 1.0)[:, None, None]
    sign_z = ((codes // 4 % 2).astype(jnp.float32) * 2.0 - 1.0)[:, None, None]
    sines = jnp.sin(theta)[:, None]
    along_x = kappa * (sines * jnp.cos(azimuth)[None, :])
    along_y = kappa * (sines * jnp.sin(azimuth)[None, :])
    along_z = kappa * jnp.cos(theta)[:, None]
    cos_x, sin_x = jnp.cos(along_x), jnp.sin(along_x)
    cos_y, sin_y = jnp.cos(along_y), jnp.sin(along_y)
    cos_z, sin_z = jnp.cos(along_z), jnp.sin(along_z)
    plane_re = cos_x * cos_y - (sign_x * sign_y) * (sin_x * sin_y)
    plane_im = sign_x * (sin_x * cos_y) + sign_y * (cos_x * sin_y)
    signed_z = sign_z * sin_z
    return (plane_re * cos_z - plane_im * signed_z, plane_re * signed_z + plane_im * cos_z)


def rotate(field, cosine, sine):
    count = field.shape[0]
    rest = field.shape[2:]
    grouped = field.reshape((count, field.shape[1] // 2, 2) + rest)
    real_part = grouped[:, :, 0]
    imag_part = grouped[:, :, 1]
    cosine = cosine[:, None]
    sine = sine[:, None]
    turned = jnp.stack(
        [real_part * cosine - imag_part * sine, real_part * sine + imag_part * cosine], axis=2
    )
    return turned.reshape(field.shape)


def body(
    patterns,
    child_code,
    box_codes,
    shift_scale,
    theta_lower,
    phi_lower,
    theta_upper,
    phi_upper,
    far_lists,
    far_kinds,
    translators,
):
    slots, parts, rows_seven, cols_seven = patterns.shape
    rows_six, cols_six = 2 * rows_seven, 2 * cols_seven
    rows_five, cols_five = 4 * rows_seven, 4 * cols_seven
    n_samp = lax.axis_size("samp")
    n_leaf = lax.axis_size("leaf")
    samp = lax.axis_index("samp")
    leaf = lax.axis_index("leaf")
    block_rows_six = rows_six // n_samp
    block_cols_six = cols_six // n_leaf
    block_rows_five = 2 * block_rows_six
    block_cols_five = 2 * block_cols_six
    halo_rows = block_rows_six + 3
    halo_cols = block_cols_six + 3
    total_six = box_codes.shape[0]
    total_five = far_lists.shape[0]
    block_size = block_rows_five * block_cols_five

    used = (child_code >= 0).astype(jnp.float32)
    codes = jnp.maximum(child_code, 0)
    rows_lower = raise_matrix(theta_lower, rows_seven)
    cols_lower = raise_matrix(phi_lower, cols_seven)
    fine = jnp.einsum("kcrq,tr->kctq", patterns, rows_lower, precision=HI)
    fine = jnp.einsum("kctq,pq->kctp", fine, cols_lower, precision=HI)
    child_cos, child_sin = phases(
        codes, shift_scale[0], iota(rows_six), iota(cols_six), rows_six, cols_six
    )
    pick_rows = halo_picker(n_samp, block_rows_six, halo_rows, rows_six)
    pick_cols = halo_picker(n_leaf, block_cols_six, halo_cols, cols_six)
    theta_block = lax.dynamic_slice_in_dim(theta_upper, samp * block_rows_five, block_rows_five)
    phi_block = lax.dynamic_slice_in_dim(phi_upper, leaf * block_cols_five, block_cols_five)
    kron = kron_matrix(theta_block, phi_block, halo_rows, halo_cols)
    parents = box_codes // KIDS
    octants = box_codes % KIDS
    top_cos, top_sin = phases(
        octants,
        shift_scale[1],
        samp * block_rows_five + iota(block_rows_five),
        leaf * block_cols_five + iota(block_cols_five),
        rows_five,
        cols_five,
    )
    top_cos = top_cos.reshape(total_six, block_size)
    top_sin = top_sin.reshape(total_six, block_size)
    members = (parents[None, :] == iota(total_five)[:, None]).astype(jnp.float32)
    entries = far_lists.reshape(-1)
    pick_source = (entries[:, None] == iota(total_five)[None, :]).astype(jnp.float32)
    kinds = far_kinds.reshape(-1)
    pick_kind = (kinds[:, None] == iota(translators.shape[0])[None, :]).astype(jnp.float32)
    operators = translators.reshape(translators.shape[0], 2, block_size)
    chosen = jnp.einsum("nk,krx->rnx", pick_kind, operators, precision=HI)

    def send(fine_part):
        comps = fine_part.shape[1]
        middle = jnp.sum(
            rotate(fine_part, child_cos, child_sin) * used[:, None, None, None], axis=0
        )
        sent = jnp.einsum("crq,sir->csiq", middle, pick_rows, precision=HI)
        sent = jnp.einsum("csiq,lkq->lscik", sent, pick_cols, precision=HI)
        sent = sent.reshape(n_leaf * n_samp, comps * halo_rows * halo_cols)
        return lax.all_to_all(sent, ("leaf", "samp"), 0, 0, tiled=True)

    def sample(arrived):
        comps = arrived.shape[1] // (halo_rows * halo_cols)
        gathered = arrived.reshape(total_six, comps, halo_rows * halo_cols).transpose(1, 0, 2)
        lifted = jnp.einsum("cbn,nx->cbx", gathered, kron, precision=HI)
        upward = jnp.einsum(
            "qb,cbx->cqx", members, turn(lifted, top_cos, top_sin), precision=HI
        )

        picked = jnp.einsum("nq,cqx->cnx", pick_source, upward, precision=HI)
        downward = turn(picked, chosen[0], chosen[1])
        downward = downward.reshape(comps, total_five, -1, block_size).sum(axis=2)

        split = jnp.einsum("qb,cqx->cbx", members, downward, precision=HI)
        split = turn(split, top_cos, -top_sin)
        shares = jnp.einsum("cbx,nx->bcn", split, kron, precision=HI)
        return shares.reshape(total_six, comps * halo_rows * halo_cols)

    def finish(returned):
        comps = returned.shape[1] // (halo_rows * halo_cols)
        returned = returned.reshape(n_leaf, n_samp, comps, halo_rows, halo_cols)
        mid_down = jnp.einsum("lscik,lkq->csiq", returned, pick_cols, precision=HI)
        mid_down = jnp.einsum("csiq,sir->crq", mid_down, pick_rows, precision=HI)

        spread = rotate(
            jnp.broadcast_to(mid_down, (slots,) + mid_down.shape), child_cos, -child_sin
        )
        incoming = jnp.einsum("kctq,tr->kcrq", spread, rows_lower, precision=HI)
        incoming = jnp.einsum("kcrp,pq->kcrq", incoming, cols_lower, precision=HI)
        return incoming * used[:, None, None, None]

    arrived = [send(fine[:, 2 * pol : 2 * pol + 2]) for pol in range(parts // 2)]
    done = []
    shares = sample(arrived[0])
    for pol in range(1, parts // 2):
        shares, next_arrived = lax.optimization_barrier((shares, arrived[pol]))
        returned = lax.all_to_all(shares, ("leaf", "samp"), 0, 0, tiled=True)
        shares = sample(next_arrived)
        finished = finish(returned)
        finished, shares = lax.optimization_barrier((finished, shares))
        done.append(finished)
    done.append(finish(lax.all_to_all(shares, ("leaf", "samp"), 0, 0, tiled=True)))
    return jnp.concatenate(done, axis=1)


def solution(mesh):
    placed = (
        P(("leaf", "samp"), None, None, None),
        P(("leaf", "samp")),
        P(),
        P(),
        P(),
        P(),
        P(),
        P(),
        P(),
        P(),
        P(None, None, "samp", "leaf"),
    )
    return jax.shard_map(
        body,
        mesh=mesh,
        in_specs=placed,
        out_specs=P(("leaf", "samp"), None, None, None),
        check_vma=False,
    )
```

```python
import math

import jax
import jax.numpy as jnp
from jax import lax
from jax.sharding import PartitionSpec as P

KIDS = 8
HI = lax.Precision.HIGH


def iota(n):
    return lax.optimization_barrier(jnp.arange(n, dtype=jnp.int32))


def raise_matrix(weights, width):
    count = weights.shape[0]
    rows = iota(count)
    columns = iota(width)
    matrix = jnp.zeros((count, width), jnp.float32)
    for stencil in range(weights.shape[1]):
        source = (rows // 2 + stencil - 1) % width
        hits = (source[:, None] == columns[None, :]).astype(jnp.float32)
        matrix = matrix + hits * weights[:, stencil][:, None]
    return matrix


def block_matrix(weights, halo):
    count = weights.shape[0]
    rows = iota(count)
    columns = iota(halo)
    matrix = jnp.zeros((count, halo), jnp.float32)
    for stencil in range(weights.shape[1]):
        hits = ((rows // 2 + stencil)[:, None] == columns[None, :]).astype(jnp.float32)
        matrix = matrix + hits * weights[:, stencil][:, None]
    return matrix


def halo_picker(blocks, block, halo, width):
    b = iota(blocks)
    i = iota(halo)
    r = iota(width)
    place = (b[:, None] * block - 1 + i[None, :]) % width
    return (place[:, :, None] == r[None, None, :]).astype(jnp.float32)


def kron_matrix(theta_block, phi_block, halo_rows, halo_cols):
    rows_five, cols_five = theta_block.shape[0], phi_block.shape[0]
    a = iota(halo_rows * halo_cols)
    b = iota(rows_five * cols_five)
    i, k = a // halo_cols, a % halo_cols
    t, p = b // cols_five, b % cols_five
    theta_rep = jnp.repeat(theta_block, cols_five, axis=0)
    phi_rep = jnp.tile(phi_block, (rows_five, 1))
    along_theta = jnp.zeros((a.shape[0], b.shape[0]), jnp.float32)
    along_phi = jnp.zeros((a.shape[0], b.shape[0]), jnp.float32)
    for stencil in range(theta_block.shape[1]):
        hit_t = (i[:, None] == (t // 2 + stencil)[None, :]).astype(jnp.float32)
        along_theta = along_theta + hit_t * theta_rep[:, stencil][None, :]
        hit_p = (k[:, None] == (p // 2 + stencil)[None, :]).astype(jnp.float32)
        along_phi = along_phi + hit_p * phi_rep[:, stencil][None, :]
    return along_theta * along_phi


def turn(field, cosine, sine):
    turned = []
    for pol in range(field.shape[0] // 2):
        re, im = field[2 * pol], field[2 * pol + 1]
        turned += [re * cosine - im * sine, re * sine + im * cosine]
    return jnp.stack(turned)


def phases(codes, kappa, theta_index, phi_index, theta_count, phi_count):
    theta = math.pi * (theta_index.astype(jnp.float32) + 0.5) / theta_count
    azimuth = 2.0 * math.pi * phi_index.astype(jnp.float32) / phi_count
    sign_x = ((codes % 2).astype(jnp.float32) * 2.0 - 1.0)[:, None, None]
    sign_y = ((codes // 2 % 2).astype(jnp.float32) * 2.0 - 1.0)[:, None, None]
    sign_z = ((codes // 4 % 2).astype(jnp.float32) * 2.0 - 1.0)[:, None, None]
    sines = jnp.sin(theta)[:, None]
    along_x = kappa * (sines * jnp.cos(azimuth)[None, :])
    along_y = kappa * (sines * jnp.sin(azimuth)[None, :])
    along_z = kappa * jnp.cos(theta)[:, None]
    cos_x, sin_x = jnp.cos(along_x), jnp.sin(along_x)
    cos_y, sin_y = jnp.cos(along_y), jnp.sin(along_y)
    cos_z, sin_z = jnp.cos(along_z), jnp.sin(along_z)
    plane_re = cos_x * cos_y - (sign_x * sign_y) * (sin_x * sin_y)
    plane_im = sign_x * (sin_x * cos_y) + sign_y * (cos_x * sin_y)
    signed_z = sign_z * sin_z
    return (plane_re * cos_z - plane_im * signed_z, plane_re * signed_z + plane_im * cos_z)


def rotate(field, cosine, sine):
    count = field.shape[0]
    rest = field.shape[2:]
    grouped = field.reshape((count, field.shape[1] // 2, 2) + rest)
    real_part = grouped[:, :, 0]
    imag_part = grouped[:, :, 1]
    cosine = cosine[:, None]
    sine = sine[:, None]
    turned = jnp.stack(
        [real_part * cosine - imag_part * sine, real_part * sine + imag_part * cosine], axis=2
    )
    return turned.reshape(field.shape)


def body(
    patterns,
    child_code,
    box_codes,
    shift_scale,
    theta_lower,
    phi_lower,
    theta_upper,
    phi_upper,
    far_lists,
    far_kinds,
    translators,
):
    slots, parts, rows_seven, cols_seven = patterns.shape
    rows_six, cols_six = 2 * rows_seven, 2 * cols_seven
    rows_five, cols_five = 4 * rows_seven, 4 * cols_seven
    n_samp = lax.axis_size("samp")
    n_leaf = lax.axis_size("leaf")
    samp = lax.axis_index("samp")
    leaf = lax.axis_index("leaf")
    block_rows_six = rows_six // n_samp
    block_cols_six = cols_six // n_leaf
    block_rows_five = 2 * block_rows_six
    block_cols_five = 2 * block_cols_six
    halo_rows = block_rows_six + 3
    halo_cols = block_cols_six + 3
    total_six = box_codes.shape[0]
    total_five = far_lists.shape[0]
    block_size = block_rows_five * block_cols_five

    used = (child_code >= 0).astype(jnp.float32)
    codes = jnp.maximum(child_code, 0)
    rows_lower = raise_matrix(theta_lower, rows_seven)
    cols_lower = raise_matrix(phi_lower, cols_seven)
    fine = jnp.einsum("kcrq,pq->kcrp", patterns, cols_lower, precision=HI)
    fine = jnp.einsum("kcrp,tr->kctp", fine, rows_lower, precision=HI)
    child_cos, child_sin = phases(
        codes, shift_scale[0], iota(rows_six), iota(cols_six), rows_six, cols_six
    )
    pick_rows = halo_picker(n_samp, block_rows_six, halo_rows, rows_six)
    pick_cols = halo_picker(n_leaf, block_cols_six, halo_cols, cols_six)
    theta_block = lax.dynamic_slice_in_dim(theta_upper, samp * block_rows_five, block_rows_five)
    phi_block = lax.dynamic_slice_in_dim(phi_upper, leaf * block_cols_five, block_cols_five)
    kron = kron_matrix(theta_block, phi_block, halo_rows, halo_cols)
    parents = box_codes // KIDS
    octants = box_codes % KIDS
    top_cos, top_sin = phases(
        octants,
        shift_scale[1],
        samp * block_rows_five + iota(block_rows_five),
        leaf * block_cols_five + iota(block_cols_five),
        rows_five,
        cols_five,
    )
    top_cos = top_cos.reshape(total_six, block_size)
    top_sin = top_sin.reshape(total_six, block_size)
    members = (parents[None, :] == iota(total_five)[:, None]).astype(jnp.float32)
    entries = far_lists.reshape(-1)
    pick_source = (entries[:, None] == iota(total_five)[None, :]).astype(jnp.float32)
    kinds = far_kinds.reshape(-1)
    pick_kind = (kinds[:, None] == iota(translators.shape[0])[None, :]).astype(jnp.float32)
    operators = translators.reshape(translators.shape[0], 2, block_size)
    chosen = jnp.einsum("nk,krx->rnx", pick_kind, operators, precision=HI)

    def polarization(fine_part):
        comps = fine_part.shape[1]
        middle = jnp.sum(
            rotate(fine_part, child_cos, child_sin) * used[:, None, None, None], axis=0
        )
        sent = jnp.einsum("crq,sir->csiq", middle, pick_rows, precision=HI)
        sent = jnp.einsum("csiq,lkq->lscik", sent, pick_cols, precision=HI)
        sent = sent.reshape(n_leaf * n_samp, comps * halo_rows * halo_cols)
        arrived = lax.all_to_all(sent, ("leaf", "samp"), 0, 0, tiled=True)

        gathered = arrived.reshape(total_six, comps, halo_rows * halo_cols).transpose(1, 0, 2)
        lifted = jnp.einsum("cbn,nx->cbx", gathered, kron, precision=HI)
        upward = jnp.einsum(
            "qb,cbx->cqx", members, turn(lifted, top_cos, top_sin), precision=HI
        )

        picked = jnp.einsum("nq,cqx->cnx", pick_source, upward, precision=HI)
        downward = turn(picked, chosen[0], chosen[1])
        downward = downward.reshape(comps, total_five, -1, block_size).sum(axis=2)

        split = jnp.einsum("qb,cqx->cbx", members, downward, precision=HI)
        split = turn(split, top_cos, -top_sin)
        shares = jnp.einsum("cbx,nx->bcn", split, kron, precision=HI)
        shares = shares.reshape(total_six, comps * halo_rows * halo_cols)
        returned = lax.all_to_all(shares, ("leaf", "samp"), 0, 0, tiled=True)
        returned = returned.reshape(n_leaf, n_samp, comps, halo_rows, halo_cols)
        mid_down = jnp.einsum("lscik,lkq->csiq", returned, pick_cols, precision=HI)
        mid_down = jnp.einsum("csiq,sir->crq", mid_down, pick_rows, precision=HI)

        spread = rotate(
            jnp.broadcast_to(mid_down, (slots,) + mid_down.shape), child_cos, -child_sin
        )
        incoming = jnp.einsum("kctq,tr->kcrq", spread, rows_lower, precision=HI)
        incoming = jnp.einsum("kcrp,pq->kcrq", incoming, cols_lower, precision=HI)
        return incoming * used[:, None, None, None]

    halves = [polarization(fine[:, 2 * pol : 2 * pol + 2]) for pol in range(parts // 2)]
    return jnp.concatenate(halves, axis=1)


def solution(mesh):
    placed = (
        P(("leaf", "samp"), None, None, None),
        P(("leaf", "samp")),
        P(),
        P(),
        P(),
        P(),
        P(),
        P(),
        P(),
        P(),
        P(None, None, "samp", "leaf"),
    )
    return jax.shard_map(
        body,
        mesh=mesh,
        in_specs=placed,
        out_specs=P(("leaf", "samp"), None, None, None),
        check_vma=False,
    )
```
